512 devices in a mesh: dp: 8 (over x, core), expert: 64 (over z, y).
Axes of the slice: x: 4, y: 4, z: 16, core: 2. Of those that a mesh axis runs over, the one named last changes fastest.
Arguments:
- grad_out: bfloat16 [65536, 2048], P(('dp', 'expert')), may hold values from -6 to 6
- gates: bfloat16 [65536, 6], P(('dp', 'expert')), may hold values from 0.049804688 to 0.59765625
- routes: int32 [65536, 6], P(('dp', 'expert')), may hold values from 0 to 63, all different within a row; in each aligned block of 128 rows (0 to 127, 128 to 255, ...) at most 16 rows name the same one
- hidden: bfloat16 [8, 64, 1024, 704], P('dp', 'expert'), may hold values from -0.23925781 to 0.23925781
- down_weight: bfloat16 [64, 704, 2048], P('expert', 'dp'), may hold values from -0.125 to 0.125
Outputs:
- grad_weight: bfloat16 [64, 704, 2048], P('expert', 'dp')
- grad_hidden: bfloat16 [8, 64, 1024, 704], P('dp', 'expert')
- grad_gates: float32 [65536, 6], P(('dp', 'expert'))
The draws below stay inside these ranges and needn't reach their ends.
Inputs may be any that keep to these rules, and one draw needn't show every extreme that they name: `routes`: each row names 6 different experts; within the rows of one device no expert is named more than 16 times, a bound that some block reaches.
All inputs are finite; a program needn't handle non-finite values.
Results may differ from the reference program's by a relative error of at most 0.017.
Values may be sent and summed in bfloat16 or wider, within the bound.
A program may use at most 64 MiB of HBM per device.

```python
import math
from functools import partial
import jax
import jax.numpy as jnp
import numpy as np
from jax import lax

D = 2048
TOP = 6
HID = 704
TOK_DEV = 128
EXPERTS = 64
CAP = 16
TOKENS = 65536
N_DP = 8
N_EXPERT = 64


def block_levels(rng, dims, cuts, low, top_value):
    def one(dim, parts):
        draws = jax.random.uniform(jax.random.fold_in(jax.random.fold_in(rng, 6), dim), (parts,), jnp.float32, low / len(cuts), top_value / len(cuts))
        return jnp.repeat(jnp.exp(draws), dims[dim] // parts).reshape((-1,) + (1,) * (len(dims) - dim - 1))

    gain = one(*cuts[0])
    for cut in cuts[1:]:
        gain = gain * one(*cut)
    return gain


def routed_block(rng, own, number, rows, count, top, most, lean):
    sequence = jax.random.permutation(rng, count)
    heavy_load, ordinary = portions_of(count, rows * top, most, lean, True), portions_of(count, rows * top, most, lean, False)
    places = jnp.arange(count)

    def named(tallies, rotation):
        used = int((tallies > 0).sum())
        fixed = max(1, used // 4)
        shifted = fixed + (places - fixed + rotation * (used - fixed)) % max(1, count - fixed)
        return jnp.zeros((count,), jnp.int32).at[sequence[jnp.where(places < fixed, places, shifted)]].set(jnp.asarray(tallies, jnp.int32))

    tallies = jnp.where(number % 4 == 0, named(heavy_load, number // 4), named(ordinary, number - number // 4 - 1))
    mixed = jax.random.permutation(jax.random.fold_in(own, 3), count)
    donor, taker = mixed[0:count // 2 * 2:2], mixed[1:count // 2 * 2:2]
    room = jnp.minimum(tallies[donor] - 1, most - tallies[taker]) // 2
    room = jnp.where((donor == sequence[0]) | (taker == sequence[0]) | (tallies[taker] == 0), 0, jnp.maximum(room, 0))
    shifted = jax.random.randint(jax.random.fold_in(own, 4), (count // 2,), 0, 1 << 20) % (room + 1)
    tallies = tallies.at[donor].add(-shifted).at[taker].add(shifted)
    items = jnp.searchsorted(jnp.cumsum(tallies), jnp.arange(rows * top), side="right").astype(jnp.int32)
    table = items.reshape(top, rows).T
    table = table[jax.random.permutation(jax.random.fold_in(own, 1), rows)]
    rotation = jax.random.randint(jax.random.fold_in(own, 2), (rows, 1), 0, top)
    return jnp.take_along_axis(table, (jnp.arange(top)[None, :] + rotation) % top, axis=1)


def portions_of(count, total, reach, lean, full):
    loads = [(1 << 20) // math.isqrt(standing ** lean) + 1 for standing in range(1, count + 1)]
    largest = reach if full else min(reach, max(-(-total // count), total * loads[0] // sum(loads)))
    least = 1 if total - largest >= count - 1 else 0
    given, rest = [largest] + [least] * (count - 1), total - largest - least * (count - 1)
    while rest > 0:
        free = [i for i in range(1, count) if given[i] < largest] or [i for i in range(1, count) if given[i] < reach]
        pool, budget = sum([loads[i] for i in free]), rest
        for i in free:
            extra = min(reach - given[i], max(1, budget * loads[i] // pool), rest)
            given[i] = given[i] + extra
            rest = rest - extra
    return np.array(given)


def normal_values(rng, extent, scale, reach, pieces=(), kind=jnp.bfloat16):
    values = jax.random.normal(rng, extent, jnp.float32) * scale
    if len(pieces) > 0:
        values = block_levels(rng, extent, pieces, -0.22, 0.18) * values
    return jnp.clip(values, min=-reach, max=reach).astype(kind)


def setup_inputs(seed: int = 0) -> dict:
    splits = jax.random.split(jax.random.key(seed), 6)
    grad_out = normal_values(splits[0], (TOKENS, D), 1.0, 6.0, ((0, 512),))
    gates = jnp.clip(0.049804688 + 0.54785156 * jax.random.uniform(splits[1], (TOKENS, TOP), jnp.float32) ** block_levels(splits[1], (TOKENS, TOP), ((0, 512),), -0.2, 0.2), 0.049804688, 0.59765625).astype(jnp.bfloat16)
    routes_keys = jax.random.split(jax.random.fold_in(splits[2], 1), TOKENS // TOK_DEV)
    routes_turns = jax.random.permutation(jax.random.fold_in(splits[2], 3), TOKENS // TOK_DEV)
    routes = jax.vmap(lambda own, number: routed_block(jax.random.fold_in(splits[2], 2), own, number, TOK_DEV, EXPERTS, TOP, CAP, 2))(routes_keys, routes_turns).reshape((TOKENS, TOP))
    hidden = normal_values(splits[3], (N_DP, EXPERTS, N_EXPERT * CAP, HID), 0.04, 0.23925781, ((0, 8), (1, 64)))
    down_weight = normal_values(splits[4], (EXPERTS, HID, D), D ** -0.5, 0.125, ((0, 64), (1, 8)))
    return {"grad_out": grad_out, "gates": gates, "routes": routes, "hidden": hidden, "down_weight": down_weight}


def group_pass(down_weight, accum, inputs):
    grad_rows, gate_rows, route_rows, saved = inputs
    owners = N_EXPERT
    flat = route_rows.reshape(owners, TOK_DEV * TOP)
    onehot = (flat[:, :, None] == jnp.arange(EXPERTS, dtype=jnp.int32)[None, None, :]).astype(jnp.int32)
    before = jnp.cumsum(onehot, axis=1) - onehot
    slot = jnp.sum(before * onehot, axis=2)
    source = jnp.arange(owners, dtype=jnp.int32)[:, None]
    target = (flat * (owners * CAP) + source * CAP + slot).reshape(-1).astype(jnp.int32)
    repeated = jnp.repeat(grad_rows, TOP, axis=0)
    rows = jnp.zeros((EXPERTS * owners * CAP, D), grad_rows.dtype).at[target].set(repeated)
    rows = rows.reshape(EXPERTS, owners * CAP, D)
    gate_slots = jnp.zeros((EXPERTS * owners * CAP,), gate_rows.dtype).at[target].set(gate_rows.reshape(-1))
    gate_slots = gate_slots.reshape(EXPERTS, owners * CAP)

    def per_expert(items):
        rows_one, gate_one, saved_one, weight_one = items
        raw = jnp.dot(rows_one, weight_one.T, preferred_element_type=jnp.float32)
        factor = gate_one.astype(jnp.float32)[:, None]
        grad_hid = (factor * raw).astype(jnp.bfloat16)
        slot_grads = jnp.sum(raw * saved_one.astype(jnp.float32), axis=1)
        scaled = (factor * rows_one.astype(jnp.float32)).astype(jnp.bfloat16)
        part_grad = jnp.dot(saved_one.T, scaled, preferred_element_type=jnp.float32).astype(jnp.bfloat16)
        return grad_hid, slot_grads, part_grad

    grad_hid, slot_grads, part_grad = lax.map(per_expert, (rows, gate_slots, saved, down_weight))
    grad_gate = slot_grads.reshape(-1)[target].reshape(owners * TOK_DEV, TOP)
    return accum + part_grad.astype(jnp.float32), (grad_hid, grad_gate)


def reference(grad_out, gates, routes, hidden, down_weight):
    group_rows = N_EXPERT * TOK_DEV
    inputs = (grad_out.reshape(N_DP, group_rows, D), gates.reshape(N_DP, group_rows, TOP),
              routes.reshape(N_DP, group_rows, TOP), hidden)
    start = jnp.zeros((EXPERTS, HID, D), jnp.float32)
    accum, outputs = lax.scan(partial(group_pass, down_weight), start, inputs)
    grad_hidden, grad_gates = outputs
    return accum.astype(jnp.bfloat16), grad_hidden, grad_gates.reshape(TOKENS, TOP)
```

```python
import jax
import jax.numpy as jnp
from jax import lax
from jax.sharding import PartitionSpec as P

NY = 4


def shards(grad_out, gates, routes, hidden, down_weight):
    owners = lax.axis_size("expert")
    token_count, chosen = routes.shape
    width = grad_out.shape[1]
    slots = hidden.shape[2]
    capacity = slots // owners
    nz = owners // NY
    columns = [[z * NY + y for z in range(nz)] for y in range(NY)]
    slabs = [[z * NY + y for y in range(NY)] for z in range(nz)]
    me = lax.axis_index("expert")
    my_y = me % NY
    my_z = me // NY

    earlier = (
        jnp.arange(token_count)[:, None] < jnp.arange(token_count)[None, :]
    ).astype(jnp.bfloat16)
    both = jnp.concatenate([routes.astype(jnp.float32), gates.astype(jnp.float32)], axis=1).T
    every = lax.all_gather(both, "expert", axis=0)
    tokens = lax.all_gather(grad_out, "expert", axis=0, axis_index_groups=columns)
    whole_weight = lax.all_gather(down_weight[0], "dp", axis=0, tiled=True)

    column = lax.dynamic_index_in_dim(
        every.reshape(nz, NY, 2 * chosen, token_count), my_y, 1, keepdims=False
    )[:, :chosen]
    named = (my_z * NY + jnp.arange(NY)).astype(jnp.float32)
    hit = jnp.any(column[:, None] == named[None, :, None, None], axis=2)
    rank = jnp.einsum(
        "sqt,tu->squ", hit.astype(jnp.bfloat16), earlier, preferred_element_type=jnp.float32
    )
    places = jnp.arange(capacity, dtype=jnp.float32)
    select = (hit[:, :, None] & (rank[:, :, None] == places[None, None, :, None])).astype(
        jnp.bfloat16
    )
    picked = jnp.einsum(
        "sct,std->scd",
        select.reshape(nz, NY * capacity, token_count),
        tokens,
        preferred_element_type=jnp.float32,
    ).astype(jnp.bfloat16)
    rows = lax.all_to_all(
        picked.reshape(nz, NY, capacity, width),
        "expert",
        split_axis=1,
        concat_axis=1,
        tiled=True,
        axis_index_groups=slabs,
    ).reshape(slots, width)

    same = every[:, :chosen] == me.astype(jnp.float32)
    mine = jnp.any(same, axis=1)
    gate_of = jnp.sum(jnp.where(same, every[:, chosen:], 0.0), axis=1)
    place = jnp.dot(mine.astype(jnp.bfloat16), earlier, preferred_element_type=jnp.float32)
    factor = jnp.sum(
        jnp.where(
            mine[:, None] & (place[:, None] == places[None, :, None]), gate_of[:, None], 0.0
        ),
        axis=2,
    ).reshape(slots, 1)

    saved = hidden[0, 0]
    contract = (((1,), (1,)), ((), ()))
    raw = lax.dot_general(rows, whole_weight, contract, preferred_element_type=jnp.float32)
    grad_hidden = (factor * raw).astype(jnp.bfloat16)
    slot_grads = jnp.sum(raw * saved.astype(jnp.float32), axis=1)
    returned = lax.all_to_all(
        slot_grads.reshape(owners, capacity), "expert", split_axis=0, concat_axis=0, tiled=True
    )
    wanted = routes[:, :, None] == jnp.arange(owners, dtype=jnp.int32)
    own = jnp.any(wanted, axis=1)
    own_rank = jnp.dot(earlier.T, own.astype(jnp.bfloat16), preferred_element_type=jnp.float32)
    slot = jnp.sum(jnp.where(wanted, own_rank[:, None], 0.0), axis=2).astype(jnp.int32)
    grad_gates = returned.reshape(-1)[routes * capacity + slot]
    scaled = (factor * rows.astype(jnp.float32)).astype(jnp.bfloat16)
    summed = lax.psum_scatter(
        lax.dot_general(
            saved, scaled, (((0,), (0,)), ((), ())), preferred_element_type=jnp.float32
        ).astype(jnp.bfloat16),
        "dp",
        scatter_dimension=0,
        tiled=True,
    )
    return (summed[None], grad_hidden[None, None], grad_gates)


def solution(mesh):
    return jax.shard_map(
        shards,
        mesh=mesh,
        in_specs=(
            P(("dp", "expert"), None),
            P(("dp", "expert"), None),
            P(("dp", "expert"), None),
            P("dp", "expert", None, None),
            P("expert", "dp", None),
        ),
        out_specs=(
            P("expert", "dp", None),
            P("dp", "expert", None, None),
            P(("dp", "expert"), None),
        ),
        check_vma=False,
    )
```

```python
import functools

import jax
import jax.numpy as jnp
from jax import lax
from jax.experimental import pallas as pl
from jax.experimental.pallas import tpu as pltpu
from jax.sharding import PartitionSpec as P

NY = 4
LANES = 128


def travel(nz, top, tokens, meta, out, buf, mbuf, pick, up_s, up_r, dn_s, dn_r,
           mu_s, mu_r, md_s, md_r, ys, yr, ls):
    me = lax.axis_index("expert")
    y = lax.rem(me, NY)
    z = lax.div(me, NY)
    count, width = tokens.shape
    half = count // 2
    cap = out.shape[1] // NY
    reach = nz // 2

    def wrap(i):
        return lax.rem(i + nz, nz)

    above = wrap(z + 1) * NY + y
    below = wrap(z - 1) * NY + y

    barrier = pltpu.get_barrier_semaphore()
    for other in [above, below] + [z * NY + lax.rem(y + j, NY) for j in range(1, NY)]:
        pl.semaphore_signal(
            barrier, inc=1, device_id={"expert": other}, device_id_type=pl.DeviceIdType.MESH
        )
    pl.semaphore_wait(barrier, NY + 1)

    def remote(src, dst, send, recv, to):
        return pltpu.make_async_remote_copy(
            src_ref=src, dst_ref=dst, send_sem=send, recv_sem=recv,
            device_id={"expert": to}, device_id_type=pl.DeviceIdType.MESH,
        )

    def piece(ref, part):
        return ref.at[pl.ds(pl.multiple_of(part * half, half), half)]

    def up(n, first=False):
        src = wrap(z - lax.div(n, 2))
        dst = piece(buf.at[src], lax.rem(n, 2))
        own = piece(tokens, lax.rem(n, 2)) if first else dst
        return remote(own, dst, up_s.at[n], up_r.at[n], above)

    def up_in(n):
        src = wrap(z - 1 - lax.div(n, 2))
        dst = piece(buf.at[src], lax.rem(n, 2))
        return remote(dst, dst, up_s.at[n], up_r.at[n], above)

    def down(n, first=False):
        src = wrap(z + lax.div(n, 2))
        dst = piece(buf.at[src], 1 - lax.rem(n, 2))
        own = piece(tokens, 1 - lax.rem(n, 2)) if first else dst
        return remote(own, dst, dn_s.at[n], dn_r.at[n], below)

    def down_in(n):
        src = wrap(z + 1 + lax.div(n, 2))
        dst = piece(buf.at[src], 1 - lax.rem(n, 2))
        return remote(dst, dst, dn_s.at[n], dn_r.at[n], below)

    def meta_up(n, first=False):
        dst = mbuf.at[wrap(z - n)]
        return remote(meta if first else dst, dst, mu_s.at[n], mu_r.at[n], above)

    def meta_up_in(n):
        dst = mbuf.at[wrap(z - 1 - n)]
        return remote(dst, dst, mu_s.at[n], mu_r.at[n], above)

    def meta_down(n, first=False):
        dst = mbuf.at[wrap(z + n)]
        return remote(meta if first else dst, dst, md_s.at[n], md_r.at[n], below)

    def meta_down_in(n):
        dst = mbuf.at[wrap(z + 1 + n)]
        return remote(dst, dst, md_s.at[n], md_r.at[n], below)

    meta_up(0, True).start()
    meta_down(0, True).start()
    for n in range(2):
        up(n, True).start()
        down(n, True).start()

    earlier = (
        lax.broadcasted_iota(jnp.int32, (count, count), 0)
        < lax.broadcasted_iota(jnp.int32, (count, count), 1)
    ).astype(jnp.bfloat16)
    places = lax.broadcasted_iota(jnp.int32, (cap, count), 0).astype(jnp.float32)

    def process(src, block, info):
        info = info.astype(jnp.float32)
        names, weights = info[:top], info[8:8 + top]
        hits, parts, gates = [], [], []
        for q in range(NY):
            same = names == (z * NY + q).astype(jnp.float32)
            hits.append(jnp.sum(jnp.where(same, 1.0, 0.0), axis=0, keepdims=True))
            gates.append(jnp.sum(jnp.where(same, weights, 0.0), axis=0, keepdims=True))
        rank = jnp.dot(
            jnp.concatenate(hits + hits, axis=0).astype(jnp.bfloat16),
            earlier,
            preferred_element_type=jnp.float32,
        )
        for q in range(NY):
            taken = (places == rank[q:q + 1]) & (hits[q] > 0.5)
            parts.append(jnp.where(taken, 1.0, 0.0))
            gate = jnp.sum(jnp.where(taken, gates[q], 0.0), axis=1, keepdims=True)
            pick[src, q * cap:(q + 1) * cap, width:] = jnp.broadcast_to(
                gate, (cap, LANES)
            ).astype(jnp.bfloat16)
        select = jnp.concatenate(parts, axis=0).astype(jnp.bfloat16)
        step = min(512, width)
        for c in range(0, width, step):
            pick[src, :, c:c + step] = jnp.dot(
                select, block[:, c:c + step], preferred_element_type=jnp.float32
            ).astype(jnp.bfloat16)

    def rows_of(ref, src, q):
        return ref.at[src, pl.ds(pl.multiple_of(q * cap, cap), cap)]

    def hand(src, j):
        q = lax.rem(y + j, NY)
        return remote(
            rows_of(pick, src, q), rows_of(out, src, y), ys.at[src, j - 1], yr.at[src, j - 1],
            z * NY + q,
        )

    def hand_in(src, j):
        q = lax.rem(y - j + NY, NY)
        return remote(
            rows_of(pick, src, q), rows_of(out, src, q), ys.at[src, j - 1], yr.at[src, j - 1],
            z * NY + q,
        )

    def keep(src):
        return pltpu.make_async_copy(rows_of(pick, src, y), rows_of(out, src, y), ls.at[src])

    def send(src):
        for j in range(1, NY):
            hand(src, j).start()
        keep(src).start()

    process(z, tokens, meta[...])

    def step(p, carry):
        for n in (2 * p, 2 * p + 1):
            up_in(n).wait_recv()
            pl.when(n + 2 <= 2 * reach - 2)(lambda n=n: up(n + 2).start())
            down_in(n).wait_recv()
            pl.when(n + 2 <= 2 * reach - 2)(lambda n=n: down(n + 2).start())
        meta_up_in(p).wait_recv()
        meta_up(p + 1).start()
        meta_down_in(p).wait_recv()
        pl.when(p + 1 <= reach - 2)(lambda: meta_down(p + 1).start())
        send(wrap(z + p))
        lower, upper = wrap(z - 1 - p), wrap(z + 1 + p)
        process(lower, buf.at[lower], mbuf[lower])
        process(upper, buf.at[upper], mbuf[upper])
        send(lower)
        return carry

    lax.fori_loop(0, reach - 1, step, 0)
    send(wrap(z + reach - 1))
    last = 2 * reach - 2
    far = wrap(z + reach)
    up_in(last).wait_recv()
    down_in(last).wait_recv()
    meta_up_in(reach - 1).wait_recv()
    process(far, buf.at[far], mbuf[far])

    for n in range(2):
        up(n, True).wait_send()
        down(n, True).wait_send()
    meta_up(0, True).wait_send()
    meta_down(0, True).wait_send()

    def sent(n, carry):
        up(n).wait_send()
        down(n).wait_send()
        return carry

    lax.fori_loop(2, 2 * reach - 1, sent, 0)

    def meta_sent(n, carry):
        meta_up(n).wait_send()
        pl.when(n <= reach - 2)(lambda: meta_down(n).wait_send())
        return carry

    lax.fori_loop(1, reach, meta_sent, 0)
    send(far)

    def done(src, carry):
        for j in range(1, NY):
            hand(src, j).wait_send()
            hand_in(src, j).wait_recv()
        keep(src).wait()
        return carry

    lax.fori_loop(0, nz, done, 0)


def bring(tokens, meta, nz, cap, top, number):
    count, width = tokens.shape
    reach = nz // 2
    full = width + LANES
    dma = pltpu.SemaphoreType.DMA
    return pl.pallas_call(
        functools.partial(travel, nz, top),
        out_shape=jax.ShapeDtypeStruct((nz, NY * cap, full), jnp.bfloat16),
        in_specs=[pl.BlockSpec(memory_space=pltpu.VMEM)] * 2,
        out_specs=pl.BlockSpec(memory_space=pl.ANY),
        scratch_shapes=[
            pltpu.VMEM((nz, count, width), jnp.bfloat16),
            pltpu.VMEM((nz,) + meta.shape, jnp.bfloat16),
            pltpu.VMEM((nz, NY * cap, full), jnp.bfloat16),
            dma((2 * reach - 1,)),
            dma((2 * reach - 1,)),
            dma((2 * reach - 1,)),
            dma((2 * reach - 1,)),
            dma((reach,)),
            dma((reach,)),
            dma((reach,)),
            dma((reach,)),
            dma((nz, NY - 1)),
            dma((nz, NY - 1)),
            dma((nz,)),
        ],
        compiler_params=pltpu.CompilerParams(
            collective_id=number, has_side_effects=True, vmem_limit_bytes=32 * 1024 * 1024
        ),
        cost_estimate=pl.CostEstimate(
            flops=2 * nz * NY * cap * count * width,
            bytes_accessed=160 * count * width * 2,
            transcendentals=0,
        ),
        name="bring_rows",
    )(tokens, meta)


def shards(grad_out, gates, routes, hidden, down_weight):
    owners = lax.axis_size("expert")
    token_count, chosen = routes.shape
    width = grad_out.shape[1]
    slots = hidden.shape[2]
    capacity = slots // owners
    nz = owners // NY

    earlier = (
        jnp.arange(token_count)[:, None] < jnp.arange(token_count)[None, :]
    ).astype(jnp.bfloat16)
    pad = jnp.zeros((8 - chosen, token_count), jnp.bfloat16)
    meta = jnp.concatenate([routes.T.astype(jnp.bfloat16), pad, gates.T, pad], axis=0)
    whole_weight = lax.all_gather(down_weight[0], "dp", axis=0, tiled=True)
    found = bring(grad_out, meta, nz, capacity, chosen, 0).reshape(slots, width + LANES)
    rows = found[:, :width]
    factor = found[:, width:width + 1].astype(jnp.float32)

    saved = hidden[0, 0]
    contract = (((1,), (1,)), ((), ()))
    raw = lax.dot_general(rows, whole_weight, contract, preferred_element_type=jnp.float32)
    grad_hidden = (factor * raw).astype(jnp.bfloat16)
    slot_grads = jnp.sum(raw * saved.astype(jnp.float32), axis=1)
    returned = lax.all_to_all(
        slot_grads.reshape(owners, capacity), "expert", split_axis=0, concat_axis=0, tiled=True
    )
    wanted = routes[:, :, None] == jnp.arange(owners, dtype=jnp.int32)
    own = jnp.any(wanted, axis=1)
    own_rank = jnp.dot(earlier.T, own.astype(jnp.bfloat16), preferred_element_type=jnp.float32)
    slot = jnp.sum(jnp.where(wanted, own_rank[:, None], 0.0), axis=2).astype(jnp.int32)
    grad_gates = returned.reshape(-1)[routes * capacity + slot]
    scaled = (factor * rows.astype(jnp.float32)).astype(jnp.bfloat16)
    summed = lax.psum_scatter(
        lax.dot_general(
            saved, scaled, (((0,), (0,)), ((), ())), preferred_element_type=jnp.float32
        ).astype(jnp.bfloat16),
        "dp",
        scatter_dimension=0,
        tiled=True,
    )
    return (summed[None], grad_hidden[None, None], grad_gates)


def solution(mesh):
    return jax.shard_map(
        shards,
        mesh=mesh,
        in_specs=(
            P(("dp", "expert"), None),
            P(("dp", "expert"), None),
            P(("dp", "expert"), None),
            P("dp", "expert", None, None),
            P("expert", "dp", None),
        ),
        out_specs=(
            P("expert", "dp", None),
            P("dp", "expert", None, None),
            P(("dp", "expert"), None),
        ),
        check_vma=False,
    )
```

```python
import functools

import jax
import jax.numpy as jnp
from jax import lax
from jax.experimental import pallas as pl
from jax.experimental.pallas import tpu as pltpu
from jax.sharding import PartitionSpec as P

NY = 4
LANES = 128


PASSES = 2
UNIT = 256
PAD = 8


def whole(nz, n_dp, top, tokens, meta, shard, saved, gw, gh, gg, buf, mbuf, pick, sel, rows,
          wall, wpad, savedp, savedg, raw, gate, partial, rs_in, sg, col, ret,
          up_s, up_r, dn_s, dn_r, mu_s, mu_r, md_s, md_r, ys, yr, ls, ws, wr, gs, gr,
          cs, cr, zs, zr):
    me = lax.axis_index("expert")
    dp = lax.axis_index("dp")
    y = lax.rem(me, NY)
    z = lax.div(me, NY)
    count, width = tokens.shape
    cap = pick.shape[1] // NY
    slots = nz * NY * cap
    depth = shard.shape[0]
    tall = depth + PAD
    reach = nz // 2
    per = 2 * reach - 1
    span = width // PASSES
    part = span // 2
    f32, bf16 = jnp.float32, jnp.bfloat16

    def wrap(i):
        return lax.rem(i + nz, nz)

    above = {"expert": wrap(z + 1) * NY + y}
    below = {"expert": wrap(z - 1) * NY + y}
    mesh_id = pl.DeviceIdType.MESH

    barrier = pltpu.get_barrier_semaphore()
    greet = [above, below] + [{"expert": z * NY + lax.rem(y + j, NY)} for j in range(1, NY)]
    greet = greet + [{"dp": lax.rem(dp + j, n_dp)} for j in range(1, n_dp)]
    for other in greet:
        pl.semaphore_signal(barrier, inc=1, device_id=other, device_id_type=mesh_id)
    pl.semaphore_wait(barrier, len(greet))

    def remote(src, dst, send, recv, to):
        return pltpu.make_async_remote_copy(
            src_ref=src, dst_ref=dst, send_sem=send, recv_sem=recv,
            device_id=to, device_id_type=mesh_id,
        )

    def own_piece(p, h):
        return tokens.at[:, pl.ds(p * span + h * part, part)]

    def up(p, n, odd, first=False):
        dst = buf.at[wrap(z - lax.div(n, 2)), p * 2 + odd]
        g = p * per + n
        return remote(own_piece(p, odd) if first else dst, dst, up_s.at[g], up_r.at[g], above)

    def up_in(p, n, odd):
        dst = buf.at[wrap(z - 1 - lax.div(n, 2)), p * 2 + odd]
        g = p * per + n
        return remote(dst, dst, up_s.at[g], up_r.at[g], above)

    def down(p, n, odd, first=False):
        dst = buf.at[wrap(z + lax.div(n, 2)), p * 2 + 1 - odd]
        g = p * per + n
        return remote(own_piece(p, 1 - odd) if first else dst, dst, dn_s.at[g], dn_r.at[g], below)

    def down_in(p, n, odd):
        dst = buf.at[wrap(z + 1 + lax.div(n, 2)), p * 2 + 1 - odd]
        g = p * per + n
        return remote(dst, dst, dn_s.at[g], dn_r.at[g], below)

    def meta_up(n, first=False):
        dst = mbuf.at[wrap(z - n)]
        return remote(meta if first else dst, dst, mu_s.at[n], mu_r.at[n], above)

    def meta_up_in(n):
        dst = mbuf.at[wrap(z - 1 - n)]
        return remote(dst, dst, mu_s.at[n], mu_r.at[n], above)

    def meta_down(n, first=False):
        dst = mbuf.at[wrap(z + n)]
        return remote(meta if first else dst, dst, md_s.at[n], md_r.at[n], below)

    def meta_down_in(n):
        dst = mbuf.at[wrap(z + 1 + n)]
        return remote(dst, dst, md_s.at[n], md_r.at[n], below)

    meta_up(0, True).start()
    meta_down(0, True).start()
    for n in range(2):
        up(0, n, n, True).start()
        down(0, n, n, True).start()

    def spread(j):
        return remote(shard, wall.at[dp], ws.at[j], wr.at[j], {"dp": lax.rem(dp + j, n_dp)})

    def spread_in(j):
        return remote(shard, wall.at[lax.rem(dp - j + n_dp, n_dp)], ws.at[j], wr.at[j],
                      {"dp": lax.rem(dp + j, n_dp)})

    for j in range(1, n_dp):
        spread(j).start()

    earlier = (
        lax.broadcasted_iota(jnp.int32, (count, count), 0)
        < lax.broadcasted_iota(jnp.int32, (count, count), 1)
    ).astype(bf16)
    places = lax.broadcasted_iota(jnp.int32, (cap, count), 0).astype(f32)

    def cols(p):
        return (0 if p == 0 else LANES + p * span), LANES + (p + 1) * span

    def choose(src, info):
        info = info.astype(f32)
        names, weights = info[:top], info[8:8 + top]
        hits, parts, gates = [], [], []
        for q in range(NY):
            same = names == (z * NY + q).astype(f32)
            hits.append(jnp.sum(jnp.where(same, 1.0, 0.0), axis=0, keepdims=True))
            gates.append(jnp.sum(jnp.where(same, weights, 0.0), axis=0, keepdims=True))
        rank = jnp.dot(
            jnp.concatenate(hits + hits, axis=0).astype(bf16), earlier,
            preferred_element_type=f32,
        )
        for q in range(NY):
            taken = (places == rank[q:q + 1]) & (hits[q] > 0.5)
            parts.append(jnp.where(taken, 1.0, 0.0))
            one = jnp.sum(jnp.where(taken, gates[q], 0.0), axis=1, keepdims=True)
            pick[src, q * cap:(q + 1) * cap, :LANES] = jnp.broadcast_to(one, (cap, LANES)).astype(
                bf16
            )
        sel[src] = jnp.concatenate(parts, axis=0).astype(bf16)

    def process(p, src, info, mine=False):
        if p == 0:
            choose(src, info)
        chosen = sel[src]
        for h in range(2):
            a = p * span + h * part
            block = tokens[:, a:a + part] if mine else buf[src, p * 2 + h]
            pick[src, :, LANES + a:LANES + a + part] = jnp.dot(
                chosen, block, preferred_element_type=f32
            ).astype(bf16)

    def rows_of(ref, p, src, q):
        a, b = cols(p)
        return ref.at[src, pl.ds(pl.multiple_of(q * cap, cap), cap), pl.ds(a, b - a)]

    def hand(p, src, j):
        q = lax.rem(y + j, NY)
        return remote(rows_of(pick, p, src, q), rows_of(rows, p, src, y),
                      ys.at[p, src, j - 1], yr.at[p, src, j - 1], {"expert": z * NY + q})

    def hand_in(p, src, j):
        q = lax.rem(y - j + NY, NY)
        return remote(rows_of(pick, p, src, q), rows_of(rows, p, src, q),
                      ys.at[p, src, j - 1], yr.at[p, src, j - 1], {"expert": z * NY + q})

    def keep(p, src):
        return pltpu.make_async_copy(rows_of(pick, p, src, y), rows_of(rows, p, src, y),
                                     ls.at[p, src])

    def send(p, src):
        for j in range(1, NY):
            hand(p, src, j).start()
        keep(p, src).start()

    def arrived(p):
        def done(src, carry):
            for j in range(1, NY):
                hand_in(p, src, j).wait_recv()
            keep(p, src).wait()
            return carry

        lax.fori_loop(0, nz, done, 0)

    def ready():
        first = (lax.broadcasted_iota(jnp.int32, (8, LANES), 1) == 0).astype(bf16)
        factor = lax.dot_general(
            first, rows[:, :, :LANES].reshape(slots, LANES), (((1,), (1,)), ((), ())),
            preferred_element_type=f32,
        )
        gate[...] = factor
        for j in range(1, n_dp):
            spread_in(j).wait_recv()
        for d in range(n_dp):
            mine = saved[d]
            savedp[d * tall:d * tall + depth] = mine
            savedp[d * tall + depth:(d + 1) * tall] = jnp.zeros((PAD, slots), bf16)
            savedg[d * tall:d * tall + depth] = (mine.astype(f32) * factor[0:1]).astype(bf16)
            savedg[d * tall + depth:(d + 1) * tall] = jnp.zeros((PAD, slots), bf16)
            wpad[d * tall + depth:(d + 1) * tall] = jnp.zeros((PAD, width), bf16)

        for d in range(n_dp):
            block = jnp.where(dp == d, shard[...], wall[d])
            wpad[d * tall:d * tall + depth] = block

    def weigh(p, u):
        a = p * span + u * UNIT
        right = rows[:, :, LANES + a:LANES + a + UNIT].reshape(slots, UNIT)
        out = jnp.dot(savedg[...], right, preferred_element_type=f32)
        for d in range(n_dp):
            partial[d, :, a:a + UNIT] = out[d * tall:d * tall + depth].astype(bf16)

    def share(p, u, j):
        a = p * span + u * UNIT
        d = lax.rem(dp + j, n_dp)
        k = p * (span // UNIT) + u
        return remote(partial.at[d, :, pl.ds(a, UNIT)], rs_in.at[dp, :, pl.ds(a, UNIT)],
                      gs.at[k, j], gr.at[k, j], {"dp": d})

    def share_in(p, u, j):
        a = p * span + u * UNIT
        d = lax.rem(dp - j + n_dp, n_dp)
        k = p * (span // UNIT) + u
        return remote(partial.at[d, :, pl.ds(a, UNIT)], rs_in.at[d, :, pl.ds(a, UNIT)],
                      gs.at[k, j], gr.at[k, j], {"dp": d})

    def give(p, u):
        for j in range(1, n_dp):
            share(p, u, j).start()

    def multiply(p, u):
        a = p * span
        lanes = slice(u * UNIT, (u + 1) * UNIT)
        few = UNIT // (NY * cap)
        right = rows[u * few:(u + 1) * few, :, LANES + a:LANES + a + span].reshape(UNIT, span)
        out = lax.dot_general(
            wpad[:, a:a + span], right, (((1,), (1,)), ((), ())), preferred_element_type=f32
        )
        if p > 0:
            out = out + raw[:, lanes]
        if p < PASSES - 1:
            raw[:, lanes] = out
            return
        scaled = out * gate[0:1, lanes]
        for d in range(n_dp):
            gh[d, :, lanes] = scaled[d * tall:d * tall + depth].astype(bf16)
        line = jnp.sum(out * savedp[:, lanes].astype(f32), axis=0, keepdims=True)
        for g in range(UNIT // LANES):
            sg[u * (UNIT // LANES) + g] = line[:, g * LANES:(g + 1) * LANES]

    wide = span // UNIT
    long = slots // UNIT
    process(0, z, meta[...], True)

    for p in range(PASSES):
        if p > 0:
            process(p, z, None, True)

        def step(i, carry, p=p):
            n = 2 * i
            up_in(p, n, 0).wait_recv()
            up(p, n + 2, 0).start()
            down_in(p, n, 0).wait_recv()
            down(p, n + 2, 0).start()
            n = n + 1
            up_in(p, n, 1).wait_recv()
            pl.when(i < reach - 2)(lambda: up(p, n + 2, 1).start())
            down_in(p, n, 1).wait_recv()
            pl.when(i < reach - 2)(lambda: down(p, n + 2, 1).start())
            if p + 1 < PASSES:
                def follow():
                    up(p + 1, 0, 0, True).start()
                    down(p + 1, 0, 0, True).start()

                pl.when(i == reach - 2)(follow)
            if p == 0:
                meta_up_in(i).wait_recv()
                meta_up(i + 1).start()
                meta_down_in(i).wait_recv()
                pl.when(i + 1 <= reach - 2)(lambda: meta_down(i + 1).start())
            send(p, wrap(z + i))
            lower, upper = wrap(z - 1 - i), wrap(z + 1 + i)
            process(p, lower, mbuf[lower] if p == 0 else None)
            process(p, upper, mbuf[upper] if p == 0 else None)
            send(p, lower)
            if p > 0:
                def begin():
                    arrived(p - 1)
                    if p == 1:
                        ready()

                pl.when(i == 1)(begin)
                for u in range(max(wide, long)):
                    def unit(u=u):
                        if u < wide:
                            weigh(p - 1, u)
                        if 0 < u <= wide:
                            give(p - 1, u - 1)
                        if u < long:
                            multiply(p - 1, u)
                        if u == max(wide, long) - 1 and u < wide:
                            give(p - 1, u)

                    pl.when(i == 2 + u)(unit)
            return carry

        lax.fori_loop(0, reach - 1, step, 0)
        send(p, wrap(z + reach - 1))
        last = per - 1
        far = wrap(z + reach)
        up_in(p, last, 0).wait_recv()
        down_in(p, last, 0).wait_recv()
        if p + 1 < PASSES:
            up(p + 1, 1, 1, True).start()
            down(p + 1, 1, 1, True).start()
        if p == 0:
            meta_up_in(reach - 1).wait_recv()
        process(p, far, mbuf[far] if p == 0 else None)
        if p == PASSES - 1:
            for n in range(2):
                for k in range(PASSES):
                    up(k, n, n, True).wait_send()
                    down(k, n, n, True).wait_send()
        send(p, far)

    own = meta[...].astype(f32)[:top]
    owner = lax.broadcasted_iota(jnp.int32, (nz * NY, count), 0).astype(f32)
    chosen = [owner == own[k:k + 1] for k in range(top)]
    taken = jnp.where(chosen[0], 1.0, 0.0)
    for k in range(1, top):
        taken = taken + jnp.where(chosen[k], 1.0, 0.0)
    own_rank = jnp.dot(taken.astype(bf16), earlier, preferred_element_type=f32)
    slot = [jnp.sum(jnp.where(chosen[k], own_rank, 0.0), axis=0, keepdims=True) for k in range(top)]

    end = PASSES - 1
    arrived(end)
    for u in range(wide):
        weigh(end, u)
        if u > 0:
            give(end, u - 1)
    for u in range(long):
        multiply(end, u)
        if u == 0:
            give(end, wide - 1)

    def cross(j):
        return remote(sg, col.at[y], cs.at[j], cr.at[j], {"expert": z * NY + lax.rem(y + j, NY)})

    def cross_in(j):
        return remote(sg, col.at[lax.rem(y - j + NY, NY)], cs.at[j], cr.at[j],
                      {"expert": z * NY + lax.rem(y + j, NY)})

    def back(j):
        s = lax.rem(z + j, nz)
        return remote(col.at[:, lax.div(s, 2)], ret.at[z], zs.at[j], zr.at[j],
                      {"expert": s * NY + y})

    def back_in(j):
        s = lax.rem(z - j + nz, nz)
        return remote(col.at[:, lax.div(s, 2)], ret.at[s], zs.at[j], zr.at[j],
                      {"expert": s * NY + y})

    for j in range(1, NY):
        cross(j).start()
    col[y] = sg[...]
    for j in range(1, NY):
        cross_in(j).wait_recv()
    lax.fori_loop(1, nz, lambda j, c: (back(j).start(), c)[1], 0)
    ret[z] = col[:, lax.div(z, 2)]

    for p in range(PASSES):
        for u in range(wide):
            for j in range(1, n_dp):
                share_in(p, u, j).wait_recv()
            a = p * span + u * UNIT
            total = partial[dp, :, a:a + UNIT].astype(f32)
            for j in range(1, n_dp):
                total = total + rs_in[lax.rem(dp + j, n_dp), :, a:a + UNIT].astype(f32)
            gw[:, a:a + UNIT] = total.astype(bf16)

    lax.fori_loop(1, nz, lambda j, c: (back_in(j).wait_recv(), c)[1], 0)
    table = ret[...].reshape(nz * NY, LANES)
    base = (lax.rem(me, LANES // cap) * cap).astype(f32)
    line = lax.broadcasted_iota(jnp.int32, (LANES, count), 0).astype(f32)
    for k in range(top):
        values = lax.dot_general(
            table, jnp.where(chosen[k], 1.0, 0.0), (((0,), (0,)), ((), ())),
            preferred_element_type=f32, precision=lax.Precision.HIGHEST,
        )
        gg[k:k + 1] = jnp.sum(
            jnp.where(line == slot[k] + base, values, 0.0), axis=0, keepdims=True
        )

    for p in range(PASSES):
        def sent(i, carry, p=p):
            for odd in range(2):
                up(p, 2 * i + odd, odd).wait_send()
                down(p, 2 * i + odd, odd).wait_send()
            return carry

        lax.fori_loop(1, reach - 1, sent, 0)
        up(p, per - 1, 0).wait_send()
        down(p, per - 1, 0).wait_send()

        def handed(src, carry, p=p):
            for j in range(1, NY):
                hand(p, src, j).wait_send()
            return carry

        lax.fori_loop(0, nz, handed, 0)
        for u in range(wide):
            for j in range(1, n_dp):
                share(p, u, j).wait_send()

    meta_up(0, True).wait_send()
    meta_down(0, True).wait_send()

    def meta_sent(n, carry):
        meta_up(n).wait_send()
        pl.when(n <= reach - 2)(lambda: meta_down(n).wait_send())
        return carry

    lax.fori_loop(1, reach, meta_sent, 0)
    for j in range(1, n_dp):
        spread(j).wait_send()
    for j in range(1, NY):
        cross(j).wait_send()
    lax.fori_loop(1, nz, lambda j, c: (back(j).wait_send(), c)[1], 0)


def shards(grad_out, gates, routes, hidden, down_weight):
    owners = lax.axis_size("expert")
    n_dp = lax.axis_size("dp")
    count, top = routes.shape
    width = grad_out.shape[1]
    slots, units = hidden.shape[2:]
    cap = slots // owners
    depth = units // n_dp
    tall = depth + PAD
    nz = owners // NY
    reach = nz // 2
    per = 2 * reach - 1
    full = width + LANES
    f32, bf16 = jnp.float32, jnp.bfloat16

    pad = jnp.zeros((8 - top, count), bf16)
    meta = jnp.concatenate([routes.T.astype(bf16), pad, gates.T, pad], axis=0)
    saved = hidden[0, 0].T.reshape(n_dp, depth, slots)
    dma = pltpu.SemaphoreType.DMA
    ring = [dma((PASSES * per,))] * 4 + [dma((reach,))] * 4
    vmem = pl.BlockSpec(memory_space=pltpu.VMEM)
    shares = width // UNIT
    gw, gh, gg = pl.pallas_call(
        functools.partial(whole, nz, n_dp, top),
        out_shape=(
            jax.ShapeDtypeStruct((depth, width), bf16),
            jax.ShapeDtypeStruct((n_dp, depth, slots), bf16),
            jax.ShapeDtypeStruct((8, count), f32),
        ),
        in_specs=[vmem] * 4,
        out_specs=(vmem, vmem, vmem),
        scratch_shapes=[
            pltpu.VMEM((nz, 2 * PASSES, count, width // (2 * PASSES)), bf16),
            pltpu.VMEM((nz,) + meta.shape, bf16),
            pltpu.VMEM((nz, NY * cap, full), bf16),
            pltpu.VMEM((nz, NY * cap, count), bf16),
            pltpu.VMEM((nz, NY * cap, full), bf16),
            pltpu.VMEM((n_dp, depth, width), bf16),
            pltpu.VMEM((n_dp * tall, width), bf16),
            pltpu.VMEM((n_dp * tall, slots), bf16),
            pltpu.VMEM((n_dp * tall, slots), bf16),
            pltpu.VMEM((n_dp * tall, slots), f32),
            pltpu.VMEM((8, slots), f32),
            pltpu.VMEM((n_dp, depth, width), bf16),
            pltpu.VMEM((n_dp, depth, width), bf16),
            pltpu.VMEM((slots // LANES, 1, LANES), f32),
            pltpu.VMEM((NY, slots // LANES, 1, LANES), f32),
            pltpu.VMEM((nz, NY, 1, LANES), f32),
        ]
        + ring
        + [dma((PASSES, nz, NY - 1))] * 2
        + [dma((PASSES, nz))]
        + [dma((n_dp,))] * 2
        + [dma((shares, n_dp))] * 2
        + [dma((NY,))] * 2
        + [dma((nz,))] * 2,
        compiler_params=pltpu.CompilerParams(
            collective_id=0, has_side_effects=True, vmem_limit_bytes=60 * 1024 * 1024
        ),
        name="routed_backward",
    )(grad_out, meta, down_weight[0], saved)
    grad_hidden = gh.reshape(units, slots).T
    return gw[None], grad_hidden[None, None], gg[:top].T


def solution(mesh):
    return jax.shard_map(
        shards,
        mesh=mesh,
        in_specs=(
            P(("dp", "expert"), None),
            P(("dp", "expert"), None),
            P(("dp", "expert"), None),
            P("dp", "expert", None, None),
            P("expert", "dp", None),
        ),
        out_specs=(
            P("expert", "dp", None),
            P("dp", "expert", None, None),
            P(("dp", "expert"), None),
        ),
        check_vma=False,
    )
```

```python
import functools

import jax
import jax.numpy as jnp
from jax import lax
from jax.experimental import pallas as pl
from jax.experimental.pallas import tpu as pltpu
from jax.sharding import PartitionSpec as P

NY = 4
LANES = 128


SPANS = (1280, 768)
PASSES = len(SPANS)
STARTS = tuple(sum(SPANS[:p]) for p in range(PASSES))
CORES = 2
TICKS = 5
UNIT = 256
PAD = 8


def whole(nz, n_dp, top, tokens, meta, shard, saved, gw, gh, gg, buf0, buf1, mbuf, pick, sel, rows,
          wall, wpad, savedp, savedg, raw, gate, partial, pair_in, both, rs_in, sg, col, ret,
          up_s, up_r, dn_s, dn_r, mu_s, mu_r, md_s, md_r, ys, yr, ls, ws, wr, gs, gr,
          ps, pr, cs, cr, zs, zr):
    me = lax.axis_index("expert")
    dp = lax.axis_index("dp")
    y = lax.rem(me, NY)
    z = lax.div(me, NY)
    count, width = tokens.shape
    cap = pick.shape[1] // NY
    slots = nz * NY * cap
    depth = shard.shape[0]
    tall = depth + PAD
    reach = nz // 2
    per = 2 * reach - 1
    bufs = (buf0, buf1)
    nx = n_dp // CORES
    core = lax.rem(dp, CORES)
    x = lax.div(dp, CORES)
    f32, bf16 = jnp.float32, jnp.bfloat16

    def wrap(i):
        return lax.rem(i + nz, nz)

    above = {"expert": wrap(z + 1) * NY + y}
    below = {"expert": wrap(z - 1) * NY + y}
    mesh_id = pl.DeviceIdType.MESH

    barrier = pltpu.get_barrier_semaphore()
    greet = [above, below] + [{"expert": z * NY + lax.rem(y + j, NY)} for j in range(1, NY)]
    greet = greet + [{"dp": lax.rem(dp + j, n_dp)} for j in range(1, n_dp)]
    for other in greet:
        pl.semaphore_signal(barrier, inc=1, device_id=other, device_id_type=mesh_id)
    pl.semaphore_wait(barrier, len(greet))

    def remote(src, dst, send, recv, to):
        return pltpu.make_async_remote_copy(
            src_ref=src, dst_ref=dst, send_sem=send, recv_sem=recv,
            device_id=to, device_id_type=mesh_id,
        )

    def own_piece(p, h):
        part = SPANS[p] // 2
        return tokens.at[:, pl.ds(pl.multiple_of(STARTS[p] + h * part, LANES), part)]

    def up(p, n, odd, first=False):
        dst = bufs[p].at[wrap(z - lax.div(n, 2)), odd]
        g = p * per + n
        return remote(own_piece(p, odd) if first else dst, dst, up_s.at[g], up_r.at[g], above)

    def up_in(p, n, odd):
        dst = bufs[p].at[wrap(z - 1 - lax.div(n, 2)), odd]
        g = p * per + n
        return remote(dst, dst, up_s.at[g], up_r.at[g], above)

    def down(p, n, odd, first=False):
        dst = bufs[p].at[wrap(z + lax.div(n, 2)), 1 - odd]
        g = p * per + n
        return remote(own_piece(p, 1 - odd) if first else dst, dst, dn_s.at[g], dn_r.at[g], below)

    def down_in(p, n, odd):
        dst = bufs[p].at[wrap(z + 1 + lax.div(n, 2)), 1 - odd]
        g = p * per + n
        return remote(dst, dst, dn_s.at[g], dn_r.at[g], below)

    def meta_up(n, first=False):
        dst = mbuf.at[wrap(z - n)]
        return remote(meta if first else dst, dst, mu_s.at[n], mu_r.at[n], above)

    def meta_up_in(n):
        dst = mbuf.at[wrap(z - 1 - n)]
        return remote(dst, dst, mu_s.at[n], mu_r.at[n], above)

    def meta_down(n, first=False):
        dst = mbuf.at[wrap(z + n)]
        return remote(meta if first else dst, dst, md_s.at[n], md_r.at[n], below)

    def meta_down_in(n):
        dst = mbuf.at[wrap(z + 1 + n)]
        return remote(dst, dst, md_s.at[n], md_r.at[n], below)

    meta_up(0, True).start()
    meta_down(0, True).start()
    for n in range(2):
        up(0, n, n, True).start()
        down(0, n, n, True).start()

    def spread(j):
        return remote(shard, wall.at[dp], ws.at[j], wr.at[j], {"dp": lax.rem(dp + j, n_dp)})

    def spread_in(j):
        return remote(shard, wall.at[lax.rem(dp - j + n_dp, n_dp)], ws.at[j], wr.at[j],
                      {"dp": lax.rem(dp + j, n_dp)})

    for j in range(1, n_dp):
        spread(j).start()

    earlier = (
        lax.broadcasted_iota(jnp.int32, (count, count), 0)
        < lax.broadcasted_iota(jnp.int32, (count, count), 1)
    ).astype(bf16)
    places = lax.broadcasted_iota(jnp.int32, (cap, count), 0).astype(f32)

    def cols(p):
        return (0 if p == 0 else LANES + STARTS[p]), LANES + STARTS[p] + SPANS[p]

    def choose(src, info):
        info = info.astype(f32)
        names, weights = info[:top], info[8:8 + top]
        hits, parts, gates = [], [], []
        for q in range(NY):
            same = names == (z * NY + q).astype(f32)
            hits.append(jnp.sum(jnp.where(same, 1.0, 0.0), axis=0, keepdims=True))
            gates.append(jnp.sum(jnp.where(same, weights, 0.0), axis=0, keepdims=True))
        rank = jnp.dot(
            jnp.concatenate(hits + hits, axis=0).astype(bf16), earlier,
            preferred_element_type=f32,
        )
        for q in range(NY):
            taken = (places == rank[q:q + 1]) & (hits[q] > 0.5)
            parts.append(jnp.where(taken, 1.0, 0.0))
            one = jnp.sum(jnp.where(taken, gates[q], 0.0), axis=1, keepdims=True)
            pick[src, q * cap:(q + 1) * cap, :LANES] = jnp.broadcast_to(one, (cap, LANES)).astype(
                bf16
            )
        sel[src] = jnp.concatenate(parts, axis=0).astype(bf16)

    def process(p, src, info, mine=False):
        if p == 0:
            choose(src, info)
        chosen = sel[src]
        part = SPANS[p] // 2
        for h in range(2):
            a = STARTS[p] + h * part
            block = tokens[:, a:a + part] if mine else bufs[p][src, h]
            pick[src, :, LANES + a:LANES + a + part] = jnp.dot(
                chosen, block, preferred_element_type=f32
            ).astype(bf16)

    def rows_of(ref, p, src, q):
        a, b = cols(p)
        return ref.at[src, pl.ds(pl.multiple_of(q * cap, cap), cap), pl.ds(a, b - a)]

    def hand(p, src, j):
        q = lax.rem(y + j, NY)
        return remote(rows_of(pick, p, src, q), rows_of(rows, p, src, y),
                      ys.at[p, src, j - 1], yr.at[p, src, j - 1], {"expert": z * NY + q})

    def hand_in(p, src, j):
        q = lax.rem(y - j + NY, NY)
        return remote(rows_of(pick, p, src, q), rows_of(rows, p, src, q),
                      ys.at[p, src, j - 1], yr.at[p, src, j - 1], {"expert": z * NY + q})

    def keep(p, src):
        return pltpu.make_async_copy(rows_of(pick, p, src, y), rows_of(rows, p, src, y),
                                     ls.at[p, src])

    def send(p, src):
        for j in range(1, NY):
            hand(p, src, j).start()
        keep(p, src).start()

    def arrived(p):
        def done(src, carry):
            for j in range(1, NY):
                hand_in(p, src, j).wait_recv()
            keep(p, src).wait()
            return carry

        lax.fori_loop(0, nz, done, 0)

    def keep_saved():
        for d in range(n_dp):
            savedp[d * tall:d * tall + depth] = saved[d]
            savedp[d * tall + depth:(d + 1) * tall] = jnp.zeros((PAD, slots), bf16)

    def keep_weight():
        for j in range(1, n_dp):
            spread_in(j).wait_recv()
        for d in range(n_dp):
            wpad[d * tall:d * tall + depth] = jnp.where(dp == d, shard[...], wall[d])
            wpad[d * tall + depth:(d + 1) * tall] = jnp.zeros((PAD, width), bf16)

    def ready():
        first = (lax.broadcasted_iota(jnp.int32, (8, LANES), 1) == 0).astype(bf16)
        factor = lax.dot_general(
            first, rows[:, :, :LANES].reshape(slots, LANES), (((1,), (1,)), ((), ())),
            preferred_element_type=f32,
        )
        gate[...] = factor
        for d in range(n_dp):
            at = slice(d * tall, (d + 1) * tall)
            savedg[at] = (savedp[at].astype(f32) * factor[0:1]).astype(bf16)

    def weigh(p, u):
        a = STARTS[p] + u * UNIT
        right = rows[:, :, LANES + a:LANES + a + UNIT].reshape(slots, UNIT)
        out = jnp.dot(savedg[...], right, preferred_element_type=f32)
        for d in range(n_dp):
            partial[d % CORES, d // CORES, :, a:a + UNIT] = out[
                d * tall:d * tall + depth
            ].astype(bf16)

    def pair(p, u):
        a = STARTS[p] + u * UNIT
        k = a // UNIT
        return remote(partial.at[1 - core, :, :, pl.ds(a, UNIT)], pair_in.at[:, :, pl.ds(a, UNIT)],
                      ps.at[k], pr.at[k], {"dp": x * CORES + 1 - core})

    def combine(p, u):
        pair(p, u).wait_recv()
        a = STARTS[p] + u * UNIT
        both[:, :, a:a + UNIT] = (
            partial[core, :, :, a:a + UNIT].astype(f32) + pair_in[:, :, a:a + UNIT].astype(f32)
        ).astype(bf16)

    def share(p, u, j):
        a = STARTS[p] + u * UNIT
        k = a // UNIT
        to = lax.rem(x + j, nx)
        return remote(both.at[to, :, pl.ds(a, UNIT)], rs_in.at[x, :, pl.ds(a, UNIT)],
                      gs.at[k, j], gr.at[k, j], {"dp": to * CORES + core})

    def share_in(p, u, j):
        a = STARTS[p] + u * UNIT
        k = a // UNIT
        near = lax.rem(x - j + nx, nx)
        return remote(both.at[near, :, pl.ds(a, UNIT)], rs_in.at[near, :, pl.ds(a, UNIT)],
                      gs.at[k, j], gr.at[k, j], {"dp": near * CORES + core})

    def tick(p, t):
        units = SPANS[p] // UNIT
        if t < units:
            weigh(p, t)
        if 0 <= t - 1 < units:
            pair(p, t - 1).start()
        if t < long:
            multiply(p, t)
        if 0 <= t - 2 < units:
            combine(p, t - 2)
        if 0 <= t - 3 < units:
            for j in range(1, nx):
                share(p, t - 3, j).start()

    def multiply(p, u):
        a, span = STARTS[p], SPANS[p]
        lanes = slice(u * UNIT, (u + 1) * UNIT)
        few = UNIT // (NY * cap)
        right = rows[u * few:(u + 1) * few, :, LANES + a:LANES + a + span].reshape(UNIT, span)
        out = lax.dot_general(
            wpad[:, a:a + span], right, (((1,), (1,)), ((), ())), preferred_element_type=f32
        )
        if p > 0:
            out = out + raw[:, lanes]
        if p < PASSES - 1:
            raw[:, lanes] = out
            return
        scaled = out * gate[0:1, lanes]
        for d in range(n_dp):
            gh[d, :, lanes] = scaled[d * tall:d * tall + depth].astype(bf16)
        line = jnp.sum(out * savedp[:, lanes].astype(f32), axis=0, keepdims=True)
        for g in range(UNIT // LANES):
            sg[u * (UNIT // LANES) + g] = line[:, g * LANES:(g + 1) * LANES]

    long = slots // UNIT
    process(0, z, meta[...], True)

    for p in range(PASSES):
        if p > 0:
            process(p, z, None, True)

        def step(i, carry, p=p):
            n = 2 * i
            up_in(p, n, 0).wait_recv()
            up(p, n + 2, 0).start()
            down_in(p, n, 0).wait_recv()
            down(p, n + 2, 0).start()
            n = n + 1
            up_in(p, n, 1).wait_recv()
            pl.when(i < reach - 2)(lambda: up(p, n + 2, 1).start())
            down_in(p, n, 1).wait_recv()
            pl.when(i < reach - 2)(lambda: down(p, n + 2, 1).start())
            if p + 1 < PASSES:
                def follow():
                    up(p + 1, 0, 0, True).start()
                    down(p + 1, 0, 0, True).start()

                pl.when(i == reach - 2)(follow)
            if p == 0:
                meta_up_in(i).wait_recv()
                meta_up(i + 1).start()
                meta_down_in(i).wait_recv()
                pl.when(i + 1 <= reach - 2)(lambda: meta_down(i + 1).start())
            send(p, wrap(z + i))
            lower, upper = wrap(z - 1 - i), wrap(z + 1 + i)
            process(p, lower, mbuf[lower] if p == 0 else None)
            process(p, upper, mbuf[upper] if p == 0 else None)
            send(p, lower)
            if p > 0:
                def begin():
                    arrived(p - 1)
                    if p == 1:
                        ready()

                if p == 1:
                    pl.when(i == 0)(keep_weight)
                pl.when(i == 1)(begin)
                for t in range(TICKS):
                    pl.when(i == 2 + t)(lambda t=t: tick(p - 1, t))
            else:
                pl.when(i == 3)(keep_saved)
            return carry

        lax.fori_loop(0, reach - 1, step, 0)
        send(p, wrap(z + reach - 1))
        if p > 0:
            for t in range(TICKS, SPANS[p - 1] // UNIT + 3):
                tick(p - 1, t)
        last = per - 1
        far = wrap(z + reach)
        up_in(p, last, 0).wait_recv()
        down_in(p, last, 0).wait_recv()
        if p + 1 < PASSES:
            up(p + 1, 1, 1, True).start()
            down(p + 1, 1, 1, True).start()
        if p == 0:
            meta_up_in(reach - 1).wait_recv()
        process(p, far, mbuf[far] if p == 0 else None)
        if p == PASSES - 1:
            for n in range(2):
                for k in range(PASSES):
                    up(k, n, n, True).wait_send()
                    down(k, n, n, True).wait_send()
        send(p, far)

    own = meta[...].astype(f32)[:top]
    owner = lax.broadcasted_iota(jnp.int32, (nz * NY, count), 0).astype(f32)
    chosen = [owner == own[k:k + 1] for k in range(top)]
    taken = jnp.where(chosen[0], 1.0, 0.0)
    for k in range(1, top):
        taken = taken + jnp.where(chosen[k], 1.0, 0.0)
    own_rank = jnp.dot(taken.astype(bf16), earlier, preferred_element_type=f32)
    slot = [jnp.sum(jnp.where(chosen[k], own_rank, 0.0), axis=0, keepdims=True) for k in range(top)]

    end = PASSES - 1
    arrived(end)
    for t in range(long):
        tick(end, t)

    def cross(j):
        return remote(sg, col.at[y], cs.at[j], cr.at[j], {"expert": z * NY + lax.rem(y + j, NY)})

    def cross_in(j):
        return remote(sg, col.at[lax.rem(y - j + NY, NY)], cs.at[j], cr.at[j],
                      {"expert": z * NY + lax.rem(y + j, NY)})

    def back(j):
        s = lax.rem(z + j, nz)
        return remote(col.at[:, lax.div(s, 2)], ret.at[z], zs.at[j], zr.at[j],
                      {"expert": s * NY + y})

    def back_in(j):
        s = lax.rem(z - j + nz, nz)
        return remote(col.at[:, lax.div(s, 2)], ret.at[s], zs.at[j], zr.at[j],
                      {"expert": s * NY + y})

    for j in range(1, NY):
        cross(j).start()
    col[y] = sg[...]
    for t in range(long, SPANS[end] // UNIT + 3):
        tick(end, t)
    for j in range(1, NY):
        cross_in(j).wait_recv()
    lax.fori_loop(1, nz, lambda j, c: (back(j).start(), c)[1], 0)
    ret[z] = col[:, lax.div(z, 2)]

    lax.fori_loop(1, nz, lambda j, c: (back_in(j).wait_recv(), c)[1], 0)
    table = ret[...].reshape(nz * NY, LANES)
    base = (lax.rem(me, LANES // cap) * cap).astype(f32)
    line = lax.broadcasted_iota(jnp.int32, (LANES, count), 0).astype(f32)
    for k in range(top):
        values = lax.dot_general(
            table, jnp.where(chosen[k], 1.0, 0.0), (((0,), (0,)), ((), ())),
            preferred_element_type=f32, precision=lax.Precision.HIGHEST,
        )
        gg[k:k + 1] = jnp.sum(
            jnp.where(line == slot[k] + base, values, 0.0), axis=0, keepdims=True
        )

    for p in range(PASSES):
        for u in range(SPANS[p] // UNIT):
            for j in range(1, nx):
                share_in(p, u, j).wait_recv()
            a = STARTS[p] + u * UNIT
            total = both[x, :, a:a + UNIT].astype(f32)
            for j in range(1, nx):
                total = total + rs_in[lax.rem(x + j, nx), :, a:a + UNIT].astype(f32)
            gw[:, a:a + UNIT] = total.astype(bf16)

    for p in range(PASSES):
        def sent(i, carry, p=p):
            for odd in range(2):
                up(p, 2 * i + odd, odd).wait_send()
                down(p, 2 * i + odd, odd).wait_send()
            return carry

        lax.fori_loop(1, reach - 1, sent, 0)
        up(p, per - 1, 0).wait_send()
        down(p, per - 1, 0).wait_send()

        def handed(src, carry, p=p):
            for j in range(1, NY):
                hand(p, src, j).wait_send()
            return carry

        lax.fori_loop(0, nz, handed, 0)
        for u in range(SPANS[p] // UNIT):
            pair(p, u).wait_send()
            for j in range(1, nx):
                share(p, u, j).wait_send()

    meta_up(0, True).wait_send()
    meta_down(0, True).wait_send()

    def meta_sent(n, carry):
        meta_up(n).wait_send()
        pl.when(n <= reach - 2)(lambda: meta_down(n).wait_send())
        return carry

    lax.fori_loop(1, reach, meta_sent, 0)
    for j in range(1, n_dp):
        spread(j).wait_send()
    for j in range(1, NY):
        cross(j).wait_send()
    lax.fori_loop(1, nz, lambda j, c: (back(j).wait_send(), c)[1], 0)


def shards(grad_out, gates, routes, hidden, down_weight):
    owners = lax.axis_size("expert")
    n_dp = lax.axis_size("dp")
    count, top = routes.shape
    width = grad_out.shape[1]
    slots, units = hidden.shape[2:]
    cap = slots // owners
    depth = units // n_dp
    tall = depth + PAD
    nz = owners // NY
    reach = nz // 2
    per = 2 * reach - 1
    full = width + LANES
    f32, bf16 = jnp.float32, jnp.bfloat16

    pad = jnp.zeros((8 - top, count), bf16)
    meta = jnp.concatenate([routes.T.astype(bf16), pad, gates.T, pad], axis=0)
    saved = hidden[0, 0].T.reshape(n_dp, depth, slots)
    dma = pltpu.SemaphoreType.DMA
    ring = [dma((PASSES * per,))] * 4 + [dma((reach,))] * 4
    vmem = pl.BlockSpec(memory_space=pltpu.VMEM)
    shares = width // UNIT
    gw, gh, gg = pl.pallas_call(
        functools.partial(whole, nz, n_dp, top),
        out_shape=(
            jax.ShapeDtypeStruct((depth, width), bf16),
            jax.ShapeDtypeStruct((n_dp, depth, slots), bf16),
            jax.ShapeDtypeStruct((8, count), f32),
        ),
        in_specs=[vmem] * 4,
        out_specs=(vmem, vmem, vmem),
        scratch_shapes=[
            pltpu.VMEM((nz, 2, count, SPANS[0] // 2), bf16),
            pltpu.VMEM((nz, 2, count, SPANS[1] // 2), bf16),
            pltpu.VMEM((nz,) + meta.shape, bf16),
            pltpu.VMEM((nz, NY * cap, full), bf16),
            pltpu.VMEM((nz, NY * cap, count), bf16),
            pltpu.VMEM((nz, NY * cap, full), bf16),
            pltpu.VMEM((n_dp, depth, width), bf16),
            pltpu.VMEM((n_dp * tall, width), bf16),
            pltpu.VMEM((n_dp * tall, slots), bf16),
            pltpu.VMEM((n_dp * tall, slots), bf16),
            pltpu.VMEM((n_dp * tall, slots), f32),
            pltpu.VMEM((8, slots), f32),
            pltpu.VMEM((CORES, n_dp // CORES, depth, width), bf16),
            pltpu.VMEM((n_dp // CORES, depth, width), bf16),
            pltpu.VMEM((n_dp // CORES, depth, width), bf16),
            pltpu.VMEM((n_dp // CORES, depth, width), bf16),
            pltpu.VMEM((slots // LANES, 1, LANES), f32),
            pltpu.VMEM((NY, slots // LANES, 1, LANES), f32),
            pltpu.VMEM((nz, NY, 1, LANES), f32),
        ]
        + ring
        + [dma((PASSES, nz, NY - 1))] * 2
        + [dma((PASSES, nz))]
        + [dma((n_dp,))] * 2
        + [dma((shares, n_dp))] * 2
        + [dma((shares,))] * 2
        + [dma((NY,))] * 2
        + [dma((nz,))] * 2,
        compiler_params=pltpu.CompilerParams(
            collective_id=0, has_side_effects=True, vmem_limit_bytes=46 * 1024 * 1024
        ),
        name="routed_backward",
    )(grad_out, meta, down_weight[0], saved)
    grad_hidden = gh.reshape(units, slots).T
    return gw[None], grad_hidden[None, None], gg[:top].T


def solution(mesh):
    return jax.shard_map(
        shards,
        mesh=mesh,
        in_specs=(
            P(("dp", "expert"), None),
            P(("dp", "expert"), None),
            P(("dp", "expert"), None),
            P("dp", "expert", None, None),
            P("expert", "dp", None),
        ),
        out_specs=(
            P("expert", "dp", None),
            P("dp", "expert", None, None),
            P(("dp", "expert"), None),
        ),
        check_vma=False,
    )
```

```python
import functools

import jax
import jax.numpy as jnp
from jax import lax
from jax.experimental import pallas as pl
from jax.experimental.pallas import tpu as pltpu
from jax.sharding import PartitionSpec as P

NY = 4
LANES = 128


SPANS = (1280, 768)
PASSES = len(SPANS)
STARTS = tuple(sum(SPANS[:p]) for p in range(PASSES))
CORES = 2
TICKS = 5
UNIT = 256
PAD = 8


def whole(nz, n_dp, top, tokens, meta, shard, saved, gw, gh, gg, buf0, buf1, mbuf, pick, sel, rows,
          saved_in, wall, wpad, savedp, savedg, raw, gate, partial, pair_in, both, rs_in, sg, col, ret,
          up_s, up_r, dn_s, dn_r, mu_s, mu_r, md_s, md_r, ys, yr, ls, ws, wr, gs, gr,
          ps, pr, cs, cr, zs, zr, fs):
    me = lax.axis_index("expert")
    dp = lax.axis_index("dp")
    y = lax.rem(me, NY)
    z = lax.div(me, NY)
    count, width = tokens.shape
    cap = pick.shape[1] // NY
    slots = nz * NY * cap
    depth = shard.shape[0]
    tall = depth + PAD
    reach = nz // 2
    per = 2 * reach - 1
    bufs = (buf0, buf1)
    nx = n_dp // CORES
    core = lax.rem(dp, CORES)
    x = lax.div(dp, CORES)
    f32, bf16 = jnp.float32, jnp.bfloat16

    def wrap(i):
        return lax.rem(i + nz, nz)

    above = {"expert": wrap(z + 1) * NY + y}
    below = {"expert": wrap(z - 1) * NY + y}
    mesh_id = pl.DeviceIdType.MESH

    barrier = pltpu.get_barrier_semaphore()
    greet = [above, below] + [{"expert": z * NY + lax.rem(y + j, NY)} for j in range(1, NY)]
    greet = greet + [{"dp": lax.rem(dp + j, n_dp)} for j in range(1, n_dp)]
    for other in greet:
        pl.semaphore_signal(barrier, inc=1, device_id=other, device_id_type=mesh_id)
    pl.semaphore_wait(barrier, len(greet))

    def remote(src, dst, send, recv, to):
        return pltpu.make_async_remote_copy(
            src_ref=src, dst_ref=dst, send_sem=send, recv_sem=recv,
            device_id=to, device_id_type=mesh_id,
        )

    def own_piece(p, h):
        part = SPANS[p] // 2
        return tokens.at[:, pl.ds(pl.multiple_of(STARTS[p] + h * part, LANES), part)]

    def up(p, n, odd, first=False):
        dst = bufs[p].at[wrap(z - lax.div(n, 2)), odd]
        g = p * per + n
        return remote(own_piece(p, odd) if first else dst, dst, up_s.at[g], up_r.at[g], above)

    def up_in(p, n, odd):
        dst = bufs[p].at[wrap(z - 1 - lax.div(n, 2)), odd]
        g = p * per + n
        return remote(dst, dst, up_s.at[g], up_r.at[g], above)

    def down(p, n, odd, first=False):
        dst = bufs[p].at[wrap(z + lax.div(n, 2)), 1 - odd]
        g = p * per + n
        return remote(own_piece(p, 1 - odd) if first else dst, dst, dn_s.at[g], dn_r.at[g], below)

    def down_in(p, n, odd):
        dst = bufs[p].at[wrap(z + 1 + lax.div(n, 2)), 1 - odd]
        g = p * per + n
        return remote(dst, dst, dn_s.at[g], dn_r.at[g], below)

    def meta_up(n, first=False):
        dst = mbuf.at[wrap(z - n)]
        return remote(meta if first else dst, dst, mu_s.at[n], mu_r.at[n], above)

    def meta_up_in(n):
        dst = mbuf.at[wrap(z - 1 - n)]
        return remote(dst, dst, mu_s.at[n], mu_r.at[n], above)

    def meta_down(n, first=False):
        dst = mbuf.at[wrap(z + n)]
        return remote(meta if first else dst, dst, md_s.at[n], md_r.at[n], below)

    def meta_down_in(n):
        dst = mbuf.at[wrap(z + 1 + n)]
        return remote(dst, dst, md_s.at[n], md_r.at[n], below)

    meta_up(0, True).start()
    meta_down(0, True).start()
    for n in range(2):
        up(0, n, n, True).start()
        down(0, n, n, True).start()

    def spread(j):
        return remote(shard, wall.at[dp], ws.at[j], wr.at[j], {"dp": lax.rem(dp + j, n_dp)})

    def spread_in(j):
        return remote(shard, wall.at[lax.rem(dp - j + n_dp, n_dp)], ws.at[j], wr.at[j],
                      {"dp": lax.rem(dp + j, n_dp)})

    for j in range(1, n_dp):
        spread(j).start()
    pltpu.make_async_copy(saved, saved_in, fs.at[0]).start()
    pltpu.make_async_copy(shard, wall.at[dp], fs.at[1]).start()

    earlier = (
        lax.broadcasted_iota(jnp.int32, (count, count), 0)
        < lax.broadcasted_iota(jnp.int32, (count, count), 1)
    ).astype(bf16)
    places = lax.broadcasted_iota(jnp.int32, (cap, count), 0).astype(f32)

    def cols(p):
        return (0 if p == 0 else LANES + STARTS[p]), LANES + STARTS[p] + SPANS[p]

    def choose(src, info):
        info = info.astype(f32)
        names, weights = info[:top], info[8:8 + top]
        hits, parts, gates = [], [], []
        for q in range(NY):
            same = names == (z * NY + q).astype(f32)
            hits.append(jnp.sum(jnp.where(same, 1.0, 0.0), axis=0, keepdims=True))
            gates.append(jnp.sum(jnp.where(same, weights, 0.0), axis=0, keepdims=True))
        rank = jnp.dot(
            jnp.concatenate(hits + hits, axis=0).astype(bf16), earlier,
            preferred_element_type=f32,
        )
        for q in range(NY):
            taken = (places == rank[q:q + 1]) & (hits[q] > 0.5)
            parts.append(jnp.where(taken, 1.0, 0.0))
            one = jnp.sum(jnp.where(taken, gates[q], 0.0), axis=1, keepdims=True)
            pick[src, q * cap:(q + 1) * cap, :LANES] = jnp.broadcast_to(one, (cap, LANES)).astype(
                bf16
            )
        sel[src] = jnp.concatenate(parts, axis=0).astype(bf16)

    def process(p, src, info, mine=False):
        if p == 0:
            choose(src, info)
        chosen = sel[src]
        part = SPANS[p] // 2
        for h in range(2):
            a = STARTS[p] + h * part
            block = tokens[:, a:a + part] if mine else bufs[p][src, h]
            pick[src, :, LANES + a:LANES + a + part] = jnp.dot(
                chosen, block, preferred_element_type=f32
            ).astype(bf16)

    def rows_of(ref, p, src, q):
        a, b = cols(p)
        return ref.at[src, pl.ds(pl.multiple_of(q * cap, cap), cap), pl.ds(a, b - a)]

    def hand(p, src, j):
        q = lax.rem(y + j, NY)
        return remote(rows_of(pick, p, src, q), rows_of(rows, p, src, y),
                      ys.at[p, src, j - 1], yr.at[p, src, j - 1], {"expert": z * NY + q})

    def hand_in(p, src, j):
        q = lax.rem(y - j + NY, NY)
        return remote(rows_of(pick, p, src, q), rows_of(rows, p, src, q),
                      ys.at[p, src, j - 1], yr.at[p, src, j - 1], {"expert": z * NY + q})

    def keep(p, src):
        return pltpu.make_async_copy(rows_of(pick, p, src, y), rows_of(rows, p, src, y),
                                     ls.at[p, src])

    def send(p, src):
        for j in range(1, NY):
            hand(p, src, j).start()
        keep(p, src).start()

    def arrived(p):
        def done(src, carry):
            for j in range(1, NY):
                hand_in(p, src, j).wait_recv()
            keep(p, src).wait()
            return carry

        lax.fori_loop(0, nz, done, 0)

    def keep_saved():
        pltpu.make_async_copy(saved, saved_in, fs.at[0]).wait()
        for d in range(n_dp):
            savedp[d * tall:d * tall + depth] = saved_in[d]
            savedp[d * tall + depth:(d + 1) * tall] = jnp.zeros((PAD, slots), bf16)

    def keep_weight():
        pltpu.make_async_copy(shard, wall.at[dp], fs.at[1]).wait()
        for j in range(1, n_dp):
            spread_in(j).wait_recv()
        for d in range(n_dp):
            wpad[d * tall:d * tall + depth] = wall[d]
            wpad[d * tall + depth:(d + 1) * tall] = jnp.zeros((PAD, width), bf16)

    def ready():
        first = (lax.broadcasted_iota(jnp.int32, (8, LANES), 1) == 0).astype(bf16)
        factor = lax.dot_general(
            first, rows[:, :, :LANES].reshape(slots, LANES), (((1,), (1,)), ((), ())),
            preferred_element_type=f32,
        )
        gate[...] = factor
        for d in range(n_dp):
            at = slice(d * tall, (d + 1) * tall)
            savedg[at] = (savedp[at].astype(f32) * factor[0:1]).astype(bf16)

    def weigh(p, u):
        a = STARTS[p] + u * UNIT
        right = rows[:, :, LANES + a:LANES + a + UNIT].reshape(slots, UNIT)
        out = jnp.dot(savedg[...], right, preferred_element_type=f32)
        for d in range(n_dp):
            partial[d % CORES, d // CORES, :, a:a + UNIT] = out[
                d * tall:d * tall + depth
            ].astype(bf16)

    def pair(p, u):
        a = STARTS[p] + u * UNIT
        k = a // UNIT
        return remote(partial.at[1 - core, :, :, pl.ds(a, UNIT)], pair_in.at[:, :, pl.ds(a, UNIT)],
                      ps.at[k], pr.at[k], {"dp": x * CORES + 1 - core})

    def combine(p, u):
        pair(p, u).wait_recv()
        a = STARTS[p] + u * UNIT
        both[:, :, a:a + UNIT] = (
            partial[core, :, :, a:a + UNIT].astype(f32) + pair_in[:, :, a:a + UNIT].astype(f32)
        ).astype(bf16)

    def share(p, u, j):
        a = STARTS[p] + u * UNIT
        k = a // UNIT
        to = lax.rem(x + j, nx)
        return remote(both.at[to, :, pl.ds(a, UNIT)], rs_in.at[x, :, pl.ds(a, UNIT)],
                      gs.at[k, j], gr.at[k, j], {"dp": to * CORES + core})

    def share_in(p, u, j):
        a = STARTS[p] + u * UNIT
        k = a // UNIT
        near = lax.rem(x - j + nx, nx)
        return remote(both.at[near, :, pl.ds(a, UNIT)], rs_in.at[near, :, pl.ds(a, UNIT)],
                      gs.at[k, j], gr.at[k, j], {"dp": near * CORES + core})

    def forward(p, t):
        units = SPANS[p] // UNIT
        if 0 <= t - 2 < units:
            combine(p, t - 2)
        if 0 <= t - 3 < units:
            for j in range(1, nx):
                share(p, t - 3, j).start()

    def tick(p, t):
        units = SPANS[p] // UNIT
        if t < units:
            weigh(p, t)
        if 0 <= t - 1 < units:
            pair(p, t - 1).start()

    def multiply(p, u):
        a, span = STARTS[p], SPANS[p]
        lanes = slice(u * UNIT, (u + 1) * UNIT)
        few = UNIT // (NY * cap)
        right = rows[u * few:(u + 1) * few, :, LANES + a:LANES + a + span].reshape(UNIT, span)
        out = lax.dot_general(
            wpad[:, a:a + span], right, (((1,), (1,)), ((), ())), preferred_element_type=f32
        )
        if p > 0:
            out = out + raw[:, lanes]
        if p < PASSES - 1:
            raw[:, lanes] = out
            return
        scaled = out * gate[0:1, lanes]
        for d in range(n_dp):
            gh[d, :, lanes] = scaled[d * tall:d * tall + depth].astype(bf16)
        line = jnp.sum(out * savedp[:, lanes].astype(f32), axis=0, keepdims=True)
        for g in range(UNIT // LANES):
            sg[u * (UNIT // LANES) + g] = line[:, g * LANES:(g + 1) * LANES]

    long = slots // UNIT
    process(0, z, meta[...], True)

    for p in range(PASSES):
        if p > 0:
            process(p, z, None, True)

        def step(i, carry, p=p):
            n = 2 * i
            up_in(p, n, 0).wait_recv()
            up(p, n + 2, 0).start()
            down_in(p, n, 0).wait_recv()
            down(p, n + 2, 0).start()
            if p == 0:
                pl.when(i == 3)(keep_saved)
            else:
                def begin():
                    arrived(p - 1)
                    if p == 1:
                        ready()

                def between(t):
                    if t < long:
                        multiply(p - 1, t)
                    forward(p - 1, t)

                if p == 1:
                    pl.when(i == 0)(keep_weight)
                pl.when(i == 1)(begin)
                for t in range(TICKS):
                    pl.when(i == 2 + t)(lambda t=t: between(t))
            n = n + 1
            up_in(p, n, 1).wait_recv()
            pl.when(i < reach - 2)(lambda: up(p, n + 2, 1).start())
            down_in(p, n, 1).wait_recv()
            pl.when(i < reach - 2)(lambda: down(p, n + 2, 1).start())
            if p + 1 < PASSES:
                def follow():
                    up(p + 1, 0, 0, True).start()
                    down(p + 1, 0, 0, True).start()

                pl.when(i == reach - 2)(follow)
            if p == 0:
                meta_up_in(i).wait_recv()
                meta_up(i + 1).start()
                meta_down_in(i).wait_recv()
                pl.when(i + 1 <= reach - 2)(lambda: meta_down(i + 1).start())
            send(p, wrap(z + i))
            lower, upper = wrap(z - 1 - i), wrap(z + 1 + i)
            process(p, lower, mbuf[lower] if p == 0 else None)
            process(p, upper, mbuf[upper] if p == 0 else None)
            send(p, lower)
            if p > 0:
                for t in range(TICKS):
                    pl.when(i == 2 + t)(lambda t=t: tick(p - 1, t))
            return carry

        lax.fori_loop(0, reach - 1, step, 0)
        send(p, wrap(z + reach - 1))
        if p > 0:
            for t in range(TICKS, SPANS[p - 1] // UNIT + 3):
                tick(p - 1, t)
                forward(p - 1, t)
        last = per - 1
        far = wrap(z + reach)
        up_in(p, last, 0).wait_recv()
        down_in(p, last, 0).wait_recv()
        if p + 1 < PASSES:
            up(p + 1, 1, 1, True).start()
            down(p + 1, 1, 1, True).start()
        if p == 0:
            meta_up_in(reach - 1).wait_recv()
        process(p, far, mbuf[far] if p == 0 else None)
        if p == PASSES - 1:
            for n in range(2):
                for k in range(PASSES):
                    up(k, n, n, True).wait_send()
                    down(k, n, n, True).wait_send()
        send(p, far)

    own = meta[...].astype(f32)[:top]
    owner = lax.broadcasted_iota(jnp.int32, (nz * NY, count), 0).astype(f32)
    chosen = [owner == own[k:k + 1] for k in range(top)]
    taken = jnp.where(chosen[0], 1.0, 0.0)
    for k in range(1, top):
        taken = taken + jnp.where(chosen[k], 1.0, 0.0)
    own_rank = jnp.dot(taken.astype(bf16), earlier, preferred_element_type=f32)
    slot = [jnp.sum(jnp.where(chosen[k], own_rank, 0.0), axis=0, keepdims=True) for k in range(top)]

    end = PASSES - 1
    arrived(end)
    for t in range(long):
        multiply(end, t)

    def cross(j):
        return remote(sg, col.at[y], cs.at[j], cr.at[j], {"expert": z * NY + lax.rem(y + j, NY)})

    def cross_in(j):
        return remote(sg, col.at[lax.rem(y - j + NY, NY)], cs.at[j], cr.at[j],
                      {"expert": z * NY + lax.rem(y + j, NY)})

    def back(j):
        s = lax.rem(z + j, nz)
        return remote(col.at[:, lax.div(s, 2)], ret.at[z], zs.at[j], zr.at[j],
                      {"expert": s * NY + y})

    def back_in(j):
        s = lax.rem(z - j + nz, nz)
        return remote(col.at[:, lax.div(s, 2)], ret.at[s], zs.at[j], zr.at[j],
                      {"expert": s * NY + y})

    for j in range(1, NY):
        cross(j).start()
    col[y] = sg[...]
    tick(end, 0)
    tick(end, 1)
    for j in range(1, NY):
        cross_in(j).wait_recv()
    lax.fori_loop(1, nz, lambda j, c: (back(j).start(), c)[1], 0)
    ret[z] = col[:, lax.div(z, 2)]

    for t in range(2, SPANS[end] // UNIT + 3):
        tick(end, t)
        forward(end, t)

    for p in range(PASSES):
        for u in range(SPANS[p] // UNIT):
            for j in range(1, nx):
                share_in(p, u, j).wait_recv()
            a = STARTS[p] + u * UNIT
            total = both[x, :, a:a + UNIT].astype(f32)
            for j in range(1, nx):
                total = total + rs_in[lax.rem(x + j, nx), :, a:a + UNIT].astype(f32)
            gw[:, a:a + UNIT] = total.astype(bf16)

    lax.fori_loop(1, nz, lambda j, c: (back_in(j).wait_recv(), c)[1], 0)
    table = ret[...].reshape(nz * NY, LANES)
    base = (lax.rem(me, LANES // cap) * cap).astype(f32)
    line = lax.broadcasted_iota(jnp.int32, (LANES, count), 0).astype(f32)
    for k in range(top):
        values = lax.dot_general(
            table, jnp.where(chosen[k], 1.0, 0.0), (((0,), (0,)), ((), ())),
            preferred_element_type=f32, precision=lax.Precision.HIGHEST,
        )
        gg[k:k + 1] = jnp.sum(
            jnp.where(line == slot[k] + base, values, 0.0), axis=0, keepdims=True
        )

    for p in range(PASSES):
        def sent(i, carry, p=p):
            for odd in range(2):
                up(p, 2 * i + odd, odd).wait_send()
                down(p, 2 * i + odd, odd).wait_send()
            return carry

        lax.fori_loop(1, reach - 1, sent, 0)
        up(p, per - 1, 0).wait_send()
        down(p, per - 1, 0).wait_send()

        def handed(src, carry, p=p):
            for j in range(1, NY):
                hand(p, src, j).wait_send()
            return carry

        lax.fori_loop(0, nz, handed, 0)
        for u in range(SPANS[p] // UNIT):
            pair(p, u).wait_send()
            for j in range(1, nx):
                share(p, u, j).wait_send()

    meta_up(0, True).wait_send()
    meta_down(0, True).wait_send()

    def meta_sent(n, carry):
        meta_up(n).wait_send()
        pl.when(n <= reach - 2)(lambda: meta_down(n).wait_send())
        return carry

    lax.fori_loop(1, reach, meta_sent, 0)
    for j in range(1, n_dp):
        spread(j).wait_send()
    for j in range(1, NY):
        cross(j).wait_send()
    lax.fori_loop(1, nz, lambda j, c: (back(j).wait_send(), c)[1], 0)


def shards(grad_out, gates, routes, hidden, down_weight):
    owners = lax.axis_size("expert")
    n_dp = lax.axis_size("dp")
    count, top = routes.shape
    width = grad_out.shape[1]
    slots, units = hidden.shape[2:]
    cap = slots // owners
    depth = units // n_dp
    tall = depth + PAD
    nz = owners // NY
    reach = nz // 2
    per = 2 * reach - 1
    full = width + LANES
    f32, bf16 = jnp.float32, jnp.bfloat16

    pad = jnp.zeros((8 - top, count), bf16)
    meta = jnp.concatenate([routes.T.astype(bf16), pad, gates.T, pad], axis=0)
    saved = hidden[0, 0].T.reshape(n_dp, depth, slots)
    dma = pltpu.SemaphoreType.DMA
    ring = [dma((PASSES * per,))] * 4 + [dma((reach,))] * 4
    vmem = pl.BlockSpec(memory_space=pltpu.VMEM)
    shares = width // UNIT
    gw, gh, gg = pl.pallas_call(
        functools.partial(whole, nz, n_dp, top),
        out_shape=(
            jax.ShapeDtypeStruct((depth, width), bf16),
            jax.ShapeDtypeStruct((n_dp, depth, slots), bf16),
            jax.ShapeDtypeStruct((8, count), f32),
        ),
        in_specs=[vmem] * 2 + [pl.BlockSpec(memory_space=pltpu.HBM)] * 2,
        out_specs=(vmem, vmem, vmem),
        scratch_shapes=[
            pltpu.VMEM((nz, 2, count, SPANS[0] // 2), bf16),
            pltpu.VMEM((nz, 2, count, SPANS[1] // 2), bf16),
            pltpu.VMEM((nz,) + meta.shape, bf16),
            pltpu.VMEM((nz, NY * cap, full), bf16),
            pltpu.VMEM((nz, NY * cap, count), bf16),
            pltpu.VMEM((nz, NY * cap, full), bf16),
            pltpu.VMEM((n_dp, depth, slots), bf16),
            pltpu.VMEM((n_dp, depth, width), bf16),
            pltpu.VMEM((n_dp * tall, width), bf16),
            pltpu.VMEM((n_dp * tall, slots), bf16),
            pltpu.VMEM((n_dp * tall, slots), bf16),
            pltpu.VMEM((n_dp * tall, slots), f32),
            pltpu.VMEM((8, slots), f32),
            pltpu.VMEM((CORES, n_dp // CORES, depth, width), bf16),
            pltpu.VMEM((n_dp // CORES, depth, width), bf16),
            pltpu.VMEM((n_dp // CORES, depth, width), bf16),
            pltpu.VMEM((n_dp // CORES, depth, width), bf16),
            pltpu.VMEM((slots // LANES, 1, LANES), f32),
            pltpu.VMEM((NY, slots // LANES, 1, LANES), f32),
            pltpu.VMEM((nz, NY, 1, LANES), f32),
        ]
        + ring
        + [dma((PASSES, nz, NY - 1))] * 2
        + [dma((PASSES, nz))]
        + [dma((n_dp,))] * 2
        + [dma((shares, n_dp))] * 2
        + [dma((shares,))] * 2
        + [dma((NY,))] * 2
        + [dma((nz,))] * 2
        + [dma((2,))],
        compiler_params=pltpu.CompilerParams(
            collective_id=0, has_side_effects=True, vmem_limit_bytes=46 * 1024 * 1024
        ),
        name="routed_backward",
    )(grad_out, meta, down_weight[0], saved)
    grad_hidden = gh.reshape(units, slots).T
    return gw[None], grad_hidden[None, None], gg[:top].T


def solution(mesh):
    return jax.shard_map(
        shards,
        mesh=mesh,
        in_specs=(
            P(("dp", "expert"), None),
            P(("dp", "expert"), None),
            P(("dp", "expert"), None),
            P("dp", "expert", None, None),
            P("expert", "dp", None),
        ),
        out_specs=(
            P("expert", "dp", None),
            P("dp", "expert", None, None),
            P(("dp", "expert"), None),
        ),
        check_vma=False,
    )
```
